128 devices in a mesh: res: 16 (over z, x), samp: 8 (over y, core).
Axes of the slice: x: 4, y: 4, z: 4, core: 2. Of those that a mesh axis runs over, the one named last changes fastest.
Arguments:
- coords_pred: float32 [32, 3, 49152], P('samp', None, 'res'), may hold values from -130 to 130
- coords_true: float32 [3, 49152], P(None, 'res'), may hold values from -55 to 55
- atom_kind: int32 [49152], P('res'), may hold values from 0 to 2
- partners: int32 [384, 5], P('res'), may hold values from 0 to 383, as said below
- noise_level: float32 [32], P('samp'), may hold values from 2 to 32
Outputs:
- copy_loss: float32 [32], P('samp')
- mean_loss: float32 [], replicated
- coord_grad: float32 [32, 3, 49152], P('samp', None, 'res')
The draws below stay inside these ranges and needn't reach their ends.
Inputs may be any that keep to these rules, and one draw needn't show every extreme that they name: `partners`: slot 0 of tile g holds g; the other used slots hold distinct tiles g' with 0 < |g' - g| <= 2, and unused slots hold g again; the pairing is symmetric (g' is listed for g exactly when g is listed for g'); some tile uses all 5 slots.
All inputs are finite; a program needn't handle non-finite values.
Results may differ from the reference program's by a relative error of at most 0.0005.
Values sent between devices are 32-bit elements; how exact they have to be, the bound alone decides.
A program may use at most 64 MiB of HBM per device.

```python
import math
import jax
import jax.numpy as jnp
from jax import lax

TILE = 128
BAND = 2
SLOTS = 5
NTILES = 384
ATOMS = 49152
COPIES = 32


def tile_chain(seed_key):
    tile_pos = (jnp.arange(ATOMS) // TILE).astype(jnp.float32)
    centre = 40.0 * jnp.stack([jnp.sin(0.11 * tile_pos), jnp.sin(0.13 * tile_pos + 1.0), jnp.sin(0.17 * tile_pos + 2.0)], axis=0)
    offsets = jnp.clip(5.0 * jax.random.normal(seed_key, (3, ATOMS), jnp.float32), -15.0, 15.0)
    return centre + offsets


def draw_coords_true(key, part):
    return tile_chain(jax.random.fold_in(key, 11)).astype(jnp.float32)


def draw_coords_pred(key, part):
    true_coords = tile_chain(jax.random.fold_in(key, 11))
    base_key = jax.random.fold_in(key, 23)
    key_axis, key_angle, key_move, key_size, key_noise = jax.random.split(base_key, 5)
    spin_axis = jax.random.normal(key_axis, (COPIES, 3), jnp.float32)
    spin_axis = spin_axis / jnp.sqrt(jnp.sum(spin_axis * spin_axis, axis=1, keepdims=True) + 1e-06)
    spin_angle = jax.random.uniform(key_angle, (COPIES,), jnp.float32, -math.pi, math.pi)
    cosine = jnp.cos(spin_angle)
    sine = jnp.sin(spin_angle)
    ux = spin_axis[:, 0]
    uy = spin_axis[:, 1]
    uz = spin_axis[:, 2]
    rest = 1.0 - cosine
    row_one = jnp.stack([cosine + ux * ux * rest, ux * uy * rest - uz * sine, ux * uz * rest + uy * sine], axis=1)
    row_two = jnp.stack([uy * ux * rest + uz * sine, cosine + uy * uy * rest, uy * uz * rest - ux * sine], axis=1)
    row_three = jnp.stack([uz * ux * rest - uy * sine, uz * uy * rest + ux * sine, cosine + uz * uz * rest], axis=1)
    spin = jnp.stack([row_one, row_two, row_three], axis=1)
    rotated = spin[:, :, 0, None] * true_coords[0] + spin[:, :, 1, None] * true_coords[1] + spin[:, :, 2, None] * true_coords[2]
    translation = jax.random.uniform(key_move, (COPIES, 3), jnp.float32, -20.0, 20.0)
    amplitude = jnp.exp(jax.random.uniform(key_size, (COPIES,), jnp.float32, math.log(0.5), math.log(3.0)))
    noise_field = jnp.clip(jax.random.normal(key_noise, (COPIES, 3, ATOMS), jnp.float32), -4.0, 4.0)
    return (rotated + translation[:, :, None] + amplitude[:, None, None] * noise_field).astype(jnp.float32)


def partner_table(seed_key):
    pair_bits = jax.random.randint(seed_key, (NTILES, BAND), 0, 2)
    full_tile = jax.random.randint(jax.random.fold_in(seed_key, 1), (), BAND, NTILES - BAND)
    tile_index = jnp.arange(NTILES, dtype=jnp.int32)[:, None]
    offset_index = jnp.arange(BAND, dtype=jnp.int32)[None, :]
    forced = (tile_index == full_tile) | (tile_index == full_tile - offset_index - 1)
    pair_bits = jnp.where(forced, 1, pair_bits)
    upper_ok = (pair_bits == 1) & (tile_index + offset_index + 1 < NTILES)
    lower_rows = jnp.clip(tile_index - offset_index - 1, 0, NTILES - 1)
    lower_bits = pair_bits[lower_rows, jnp.broadcast_to(offset_index, (NTILES, BAND))]
    lower_ok = (lower_bits == 1) & (tile_index - offset_index - 1 >= 0)
    candidates = jnp.concatenate([tile_index, tile_index + offset_index + 1, tile_index - offset_index - 1], axis=1)
    present = jnp.concatenate([jnp.ones((NTILES, 1), jnp.int32), upper_ok.astype(jnp.int32), lower_ok.astype(jnp.int32)], axis=1)
    sort_keys = (1 - present) * SLOTS + jnp.arange(SLOTS, dtype=jnp.int32)[None, :]
    slot_order = jnp.argsort(sort_keys, axis=1)
    sorted_tiles = jnp.take_along_axis(candidates, slot_order, axis=1)
    sorted_present = jnp.take_along_axis(present, slot_order, axis=1)
    return jnp.where(sorted_present == 1, sorted_tiles, tile_index).astype(jnp.int32)


def draw_partners(key, part):
    return partner_table(jax.random.fold_in(key, 5))


def place_ends(drawn, rng, least, high):
    shape = drawn.shape
    index_at = [jax.random.randint(jax.random.fold_in(rng, axis), (), 0, shape[axis]) for axis in range(len(shape))]
    drawn = drawn.at[tuple(index_at)].set(least)
    longest = shape.index(max(shape))
    index_at[longest] = (index_at[longest] + 1) % shape[longest]
    return drawn.at[tuple(index_at)].set(high)


def block_scale(stream_key, extent, shards, least, top_value):
    gain, own = 1.0, jax.random.fold_in(stream_key, 6)
    for dim, blocks in shards:
        heights = jnp.exp(jax.random.uniform(jax.random.fold_in(own, dim), (blocks,), jnp.float32, least / len(shards), top_value / len(shards)))
        gain = gain * jnp.repeat(heights, extent[dim] // blocks).reshape([-1 if axis == dim else 1 for axis in range(len(extent))])
    return gain


def setup_inputs(seed: int = 0) -> dict:
    seeds = jax.random.split(jax.random.key(seed), 6)
    return {
        "coords_pred": draw_coords_pred(jax.random.fold_in(seeds[5], 71), 0),
        "coords_true": draw_coords_true(jax.random.fold_in(seeds[5], 71), 0),
        "atom_kind": place_ends(jax.random.randint(seeds[2], (ATOMS,), 0, 3), jax.random.fold_in(seeds[2], 1), 0, 2).astype(jnp.int32),
        "partners": draw_partners(jax.random.fold_in(seeds[5], 71), 0),
        "noise_level": jnp.clip(jnp.exp(math.log(32.0) - 2.7725887 * jax.random.uniform(seeds[4], (COPIES,), jnp.float32) ** block_scale(seeds[4], (COPIES,), ((0, 8),), -0.2, 0.2)), 2.0, 32.0),
    }


precise = lax.Precision.HIGHEST
thresholds = (0.5, 1.0, 2.0, 4.0)
sigma_data = 16.0

def atom_weight(atom_kind):
    return jnp.where(atom_kind == 1, 5.0, jnp.where(atom_kind == 2, 10.0, 1.0)).astype(jnp.float32)

def atom_cutoff(atom_kind):
    return jnp.where(atom_kind == 1, 30.0, 15.0).astype(jnp.float32)

def moments(coords_pred, coords_true, weight):
    weight_sum = jnp.sum(weight)
    pred_sum = jnp.einsum('sca,a->sc', coords_pred, weight, precision=precise)
    true_sum = jnp.einsum('ca,a->c', coords_true, weight, precision=precise)
    cross = jnp.einsum('sca,da->scd', coords_pred * weight, coords_true, precision=precise)
    return (weight_sum, pred_sum, true_sum, cross)

def rotation_of(weight_sum, pred_sum, true_sum, cross):
    pred_mean = pred_sum / weight_sum
    true_mean = true_sum / weight_sum
    covariance = cross - pred_sum[:, :, None] * true_mean[None, None, :]
    frobenius = jnp.sqrt(lax.optimization_barrier(jnp.sum(covariance * covariance, axis=(1, 2))))
    polar_factor = covariance / frobenius[:, None, None]
    for sweep_index in range(20):
        gram_matrix = jnp.einsum('sab,scb->sac', polar_factor, polar_factor, precision=precise)
        polar_factor = 1.5 * polar_factor - 0.5 * jnp.einsum('sac,scd->sad', gram_matrix, polar_factor, precision=precise)
    return (polar_factor, pred_mean, true_mean)

def aligned_truth(rotation, pred_mean, true_mean, coords_true):
    centred = coords_true - true_mean[:, None]
    return jnp.einsum('scd,da->sca', rotation, centred, precision=precise) + pred_mean[:, :, None]

def pair_terms(own_rows, partner_rows, own_tile, partner_tiles, copies):
    tile_len = own_rows.shape[-1]
    slot_count = partner_tiles.shape[0]
    own_pred = own_rows[:3 * copies].reshape(copies, 3, tile_len)
    own_true = own_rows[3 * copies:3 * copies + 3]
    own_cut = own_rows[3 * copies + 3]
    far_pred = partner_rows[:3 * copies].reshape(copies, 3, slot_count, tile_len)
    far_true = partner_rows[3 * copies:3 * copies + 3]
    far_cut = partner_rows[3 * copies + 3]
    pred_terms = []
    true_terms = []
    for component in range(3):
        coord_gap = own_pred[:, component, None, :, None] - far_pred[:, component, :, None, :]
        pred_terms.append(coord_gap * coord_gap)
        true_gap = own_true[component][None, :, None] - far_true[component][:, None, :]
        true_terms.append(true_gap * true_gap)
    pred_dist = jnp.sqrt(pred_terms[0] + pred_terms[1] + pred_terms[2] + 1e-06)
    true_dist = jnp.sqrt(true_terms[0] + true_terms[1] + true_terms[2] + 1e-06)
    slot_used = (jnp.arange(slot_count) == 0) | (partner_tiles != own_tile)
    same_atom = jnp.arange(tile_len)[:, None] == jnp.arange(tile_len)[None, :]
    diagonal = (partner_tiles == own_tile)[:, None, None] & same_atom[None]
    usable = slot_used[:, None, None] & jnp.logical_not(diagonal)
    mask_fwd = jnp.where(usable & (true_dist < far_cut[:, None, :]), 1.0, 0.0).astype(jnp.float32)
    mask_back = jnp.where(usable & (true_dist < own_cut[None, :, None]), 1.0, 0.0).astype(jnp.float32)
    spread = jnp.abs(pred_dist - true_dist)
    score_parts = []
    slope_parts = []
    for threshold in thresholds:
        squash = jax.nn.sigmoid(threshold - spread)
        score_parts.append(squash)
        slope_parts.append(squash * (1.0 - squash))
    pair_score = 0.25 * (score_parts[0] + score_parts[1] + score_parts[2] + score_parts[3])
    pair_slope = -0.25 * (slope_parts[0] + slope_parts[1] + slope_parts[2] + slope_parts[3])
    pair_count = jnp.sum(mask_fwd)
    score_sum = lax.optimization_barrier(jnp.sum(mask_fwd * pair_score, axis=(1, 2, 3)))
    factor = (mask_fwd + mask_back) * pair_slope * jnp.sign(pred_dist - true_dist) / pred_dist
    weight_row = lax.optimization_barrier(jnp.sum(factor, axis=(1, 3)))
    pull_parts = []
    for component in range(3):
        remote = jnp.einsum('skij,skj->si', factor, far_pred[:, component], precision=precise)
        pull_parts.append(own_pred[:, component] * weight_row - remote)
    return (pair_count, score_sum, jnp.stack(pull_parts, axis=1))

def reference(coords_pred, coords_true, atom_kind, partners, noise_level):
    copies = coords_pred.shape[0]
    atom_total = coords_pred.shape[2]
    weight = atom_weight(atom_kind)
    cutoff = atom_cutoff(atom_kind)
    weight_sum, pred_sum, true_sum, cross = moments(coords_pred, coords_true, weight)
    rotation, pred_mean, true_mean = rotation_of(weight_sum, pred_sum, true_sum, cross)
    target = aligned_truth(rotation, pred_mean, true_mean, coords_true)
    deviation = coords_pred - target
    square_err = lax.optimization_barrier(jnp.sum(weight * deviation * deviation, axis=(1, 2)))
    packed = jnp.concatenate([coords_pred.reshape(3 * copies, atom_total), coords_true, cutoff[None]], axis=0)
    tile_rows = packed.reshape(packed.shape[0], NTILES, TILE)

    def one_tile(tile_id):
        own_rows = lax.dynamic_index_in_dim(tile_rows, tile_id, 1, keepdims=False)
        partner_tiles = lax.dynamic_index_in_dim(partners, tile_id, 0, keepdims=False)
        partner_rows = jnp.take(tile_rows, partner_tiles, axis=1)
        return pair_terms(own_rows, partner_rows, tile_id, partner_tiles, copies)
    counts, scores, pull_tiles = lax.map(one_tile, jnp.arange(NTILES, dtype=jnp.int32))
    pair_total = jnp.sum(counts)
    score_total = lax.optimization_barrier(jnp.sum(scores, axis=0))
    pull_field = jnp.moveaxis(pull_tiles, 0, 2).reshape(copies, 3, atom_total)
    loss_weight = (noise_level * noise_level + sigma_data * sigma_data) / (noise_level * sigma_data * (noise_level * sigma_data))
    mean_square = square_err / (3.0 * weight_sum)
    copy_loss = loss_weight * mean_square + 1.0 - score_total / pair_total
    mean_loss = jnp.mean(copy_loss)
    grad_scale = 16.0 * atom_total
    coord_grad = grad_scale * (2.0 * loss_weight[:, None, None] * weight * deviation / (3.0 * weight_sum) - pull_field / pair_total)
    return (copy_loss, mean_loss, coord_grad)
```

```python
import functools

import jax
import jax.numpy as jnp
from jax import lax
from jax.experimental import pallas as pl
from jax.experimental.pallas import tpu as pltpu
from jax.sharding import PartitionSpec as P

F32, BF16 = jnp.float32, jnp.bfloat16
MESH = pl.DeviceIdType.MESH
TILE = 128
BAND = 2
CHUNK = 16
PARTS = 16
LEVELS = (0.25, 0.5, 1.0, 2.0)
STEEP = 1e15
SIGMA = 16.0
VMEM_BYTES = 56 * 1024 * 1024


def lanes(tile, count=1):
    return pl.ds(pl.multiple_of(tile * TILE, TILE), count * TILE)


def atom_weight(kind):
    return jnp.where(kind == 1, 5.0, jnp.where(kind == 2, 10.0, 1.0)).astype(F32)


def pieces(x):
    high = x.astype(BF16).astype(F32)
    mid = (x - high).astype(BF16).astype(F32)
    return high, mid, (x - high) - mid


def fill_rows(rows, split, moved, at, pred, true, kind):
    copies, _, width = pred.shape
    span = pl.ds(at, width)
    for s in range(copies):
        half = 0.5 * pred[s]
        rows[3 * s : 3 * s + 3, span] = half
        unit = jnp.concatenate([jnp.ones((1, width), F32), jnp.zeros((4, width), F32)], axis=0)
        parts = pieces(jnp.concatenate([half, unit], axis=0))
        stack = jnp.concatenate([*parts, jnp.zeros((8, width), F32)], axis=0)
        moved[s, :, span] = stack.astype(BF16)
    rows[3 * copies : 3 * copies + 3, span] = 0.5 * true[...]
    rows[3 * copies + 3 : 3 * copies + 4, span] = jnp.where(kind[...] == 1, 15.0, 7.5).astype(F32)
    if split is not None:
        high, mid, low = pieces(rows[:, span])
        split[0:PARTS, span] = high
        split[PARTS : 2 * PARTS, span] = mid
        split[2 * PARTS : 3 * PARTS, span] = low


def fill_select(select):
    row = lax.broadcasted_iota(jnp.int32, select.shape, 0) % PARTS
    column = lax.broadcasted_iota(jnp.int32, select.shape, 1) // TILE
    select[...] = jnp.where(row == column, 1.0, 0.0).astype(BF16)


def spread_steps(split, select, wide, slot, tile):
    turned = jnp.transpose(split[:, lanes(tile)]).astype(BF16)

    def step(k):
        part = slice(2 * k * TILE, 2 * (k + 1) * TILE)
        wide[slot, :, part] = jnp.dot(turned, select[:, part], preferred_element_type=F32)

    return [functools.partial(step, k) for k in range(PARTS // 2)]


def masks(rows, near, wide, slot, dist, mask, flag=None, own=False):
    copies = (PARTS - 4) // 3
    true = [rows[3 * copies + c : 3 * copies + c + 1, near] for c in range(3)]
    cut = rows[3 * copies + 3 : 3 * copies + 4, near]
    count = jnp.zeros((8, TILE), F32)

    def wide_row(r, band):
        return wide[slot, band, r * TILE : (r + 1) * TILE]

    for start in range(0, TILE, CHUNK):
        band = slice(start, start + CHUNK)
        gap = [wide_row(3 * copies + c, band) - true[c] for c in range(3)]
        square = gap[0] * gap[0] + gap[1] * gap[1] + (gap[2] * gap[2] + 2.5e-7)
        length = square * lax.rsqrt(square)
        both = jnp.where(length < cut, 1.0, 0.0) + jnp.where(
            length < wide_row(3 * copies + 3, band), 1.0, 0.0
        )
        if own:
            row = lax.broadcasted_iota(jnp.int32, (CHUNK, TILE), 0) + start
            both = jnp.where(row == lax.broadcasted_iota(jnp.int32, (CHUNK, TILE), 1), 0.0, both)
        if flag is not None:
            both = both * flag
        dist[band] = length
        mask[band] = both
        for v in range(0, CHUNK, 8):
            count += both[v : v + 8]
    return count


def forces(rows, near, s, wide, slot, dist, mask, force, fillers):
    mate = [rows[3 * s + c : 3 * s + c + 1, near] for c in range(3)]
    total = jnp.zeros((8, TILE), F32)
    for start in range(0, TILE, CHUNK):
        band = slice(start, start + CHUNK)
        gap = [
            wide[slot, band, (3 * s + c) * TILE : (3 * s + c + 1) * TILE] - mate[c] for c in range(3)
        ]
        square = gap[0] * gap[0] + gap[1] * gap[1] + (gap[2] * gap[2] + 2.5e-7)
        inverse = lax.rsqrt(square)
        excess = square * inverse - dist[band]
        spread = jnp.abs(excess)
        th = [jnp.tanh(level - spread) for level in LEVELS]
        both = mask[band]
        score = both * ((th[0] + th[1]) + (th[2] + th[3]))
        for v in range(0, CHUNK, 8):
            total += score[v : v + 8]
        slope = 4.0 - ((th[0] * th[0] + th[1] * th[1]) + (th[2] * th[2] + th[3] * th[3]))
        pull = ((both * inverse) * jnp.tanh(excess * STEEP)) * slope
        high = pull.astype(BF16)
        force[s, band, 0:TILE] = high
        force[s, band, TILE : 2 * TILE] = (pull - high.astype(F32)).astype(BF16)
        if fillers:
            fillers.pop(0)()
    return total


def fold(x):
    return (x[0:8] + x[8:16]) + x[16:24]


def down(moved, s, span, force):
    out = jnp.dot(moved[s, :, span], force[s], preferred_element_type=F32)
    return fold(out[:, 0:TILE] + out[:, TILE : 2 * TILE])


def across(moved, s, span, force):
    block = moved[s, :, span]
    return fold(
        lax.dot_general(
            jnp.concatenate([block, block], axis=1),
            force[s],
            (((1,), (1,)), ((), ())),
            preferred_element_type=F32,
        )
    )


def inner_kernel(
    pred, true, kind, partners, acc, sums, rows, split, moved, select, wide, dist, mask, force, pairs
):
    copies, _, atoms = pred.shape
    tiles = atoms // TILE
    first = lax.axis_index("res") * tiles

    def look(g, n):
        for k in range(1, partners.shape[1]):
            q = partners[g, k] - first
            pairs[n] = g
            pairs[n + 1] = q
            n = n + jnp.where((q > g) & (q < tiles), 2, 0)
        return n

    count = lax.fori_loop(0, tiles, look, 0)
    pairs[count] = 0
    fill_rows(rows, split, moved, 0, pred, true, kind)
    fill_select(select)
    acc[...] = jnp.zeros_like(acc)
    sums[...] = jnp.zeros_like(sums)
    for step in spread_steps(split, select, wide, 0, pairs[0]):
        step()

    def visit(p, carry):
        g, q, later = pairs[2 * p], pairs[2 * p + 1], pairs[2 * p + 2]
        slot = lax.rem(p, 2)
        near, span = lanes(q), lanes(g)
        fillers = []
        for step in spread_steps(split, select, wide, 1 - slot, later):
            fillers += [step, lambda: None, lambda: None]
        sums[0] += masks(rows, near, wide, slot, dist, mask)
        for s in range(copies):
            sums[1 + s] += forces(rows, near, s, wide, slot, dist, mask, force, fillers)
            acc[q, s] += down(moved, s, span, force)
            acc[g, s] += across(moved, s, near, force)
        return carry

    lax.fori_loop(0, count // 2, visit, 0)


def outer_kernel(
    res,
    samp,
    pred,
    true,
    kind,
    partners,
    noise,
    inner,
    inner_sums,
    copy_loss,
    mean_loss,
    grad,
    rows,
    moved,
    split,
    select,
    wide,
    dist,
    mask,
    force,
    acc,
    sums,
    halo_pred,
    halo_true,
    halo_kind,
    back,
    back_in,
    moment,
    moments,
    part,
    parts,
    loss,
    losses,
    turn,
    deviation,
    halo_send,
    halo_recv,
    back_send,
    back_recv,
    moment_send,
    moment_recv,
    part_send,
    part_recv,
    loss_send,
    loss_recv,
):
    copies, _, atoms = pred.shape
    tiles = atoms // TILE
    r, v = lax.axis_index("res"), lax.axis_index("samp")
    left, right = lax.rem(r + res - 1, res), lax.rem(r + 1, res)

    barrier = pltpu.get_barrier_semaphore()

    def greet_res(k, carry):
        pl.semaphore_signal(
            barrier, inc=1, device_id=(lax.rem(r + k, res), v), device_id_type=MESH
        )
        return carry

    def greet_samp(k, carry):
        pl.semaphore_signal(
            barrier, inc=1, device_id=(r, lax.rem(v + k, samp)), device_id_type=MESH
        )
        return carry

    lax.fori_loop(1, res, greet_res, 0)
    lax.fori_loop(1, samp, greet_samp, 0)

    fill_rows(rows, split, moved, 0, pred, true, kind)
    fill_select(select)
    weight = atom_weight(kind[...])
    lane = lax.broadcasted_iota(jnp.int32, (4, TILE), 1)
    for s in range(copies):
        block = jnp.concatenate([pred[s], jnp.ones((1, atoms), F32)], axis=0)
        packed = jnp.zeros((4, TILE), F32)
        for k in range(4):
            by = weight if k == 0 else weight * true[k - 1 : k, :]
            packed = jnp.where(lane == k, jnp.sum(block * by, axis=1, keepdims=True), packed)
        moment[4 * s : 4 * s + 4, :] = packed

    acc[...] = inner[...]
    sums[...] = jnp.zeros_like(sums)
    for step in spread_steps(split, select, wide, 0, 0):
        step()

    def visit_own(g, carry):
        slot = lax.rem(g, 2)
        near = lanes(g)
        fillers = []
        for step in spread_steps(split, select, wide, 1 - slot, lax.rem(g + 1, tiles)):
            fillers += [step, lambda: None, lambda: None]
        sums[0] += masks(rows, near, wide, slot, dist, mask, own=True)
        for s in range(copies):
            sums[1 + s] += forces(rows, near, s, wide, slot, dist, mask, force, fillers)
            acc[g, s] += down(moved, s, near, force)
        return carry

    early = tiles // 4
    lax.fori_loop(0, early, visit_own, 0)

    pl.semaphore_wait(barrier, res - 1 + samp - 1)

    edge = pl.ds(0, BAND * TILE)
    halo = [
        pltpu.make_async_remote_copy(
            src_ref=source,
            dst_ref=target,
            send_sem=halo_send.at[k],
            recv_sem=halo_recv.at[k],
            device_id=(left, v),
            device_id_type=MESH,
        )
        for k, (source, target) in enumerate(
            [
                (pred.at[:, :, edge], halo_pred),
                (true.at[:, edge], halo_true),
                (kind.at[:, edge], halo_kind),
            ]
        )
    ]
    for copy in halo:
        copy.start()

    def to_res(source, target, send, recv, k):
        peer = lax.rem(r + k, res)
        return pltpu.make_async_remote_copy(
            src_ref=source,
            dst_ref=target.at[r],
            send_sem=send.at[k],
            recv_sem=recv.at[r],
            device_id=(peer, v),
            device_id_type=MESH,
        )

    def from_res(source, target, send, recv, k):
        peer = lax.rem(r + k, res)
        return pltpu.make_async_remote_copy(
            src_ref=source,
            dst_ref=target.at[peer],
            send_sem=send.at[k],
            recv_sem=recv.at[peer],
            device_id=(peer, v),
            device_id_type=MESH,
        )

    def start_res(source, target, send, recv):
        def body(k, carry):
            to_res(source, target, send, recv, k).start()
            return carry

        lax.fori_loop(1, res, body, 0)

    def wait_res(source, target, send, recv):
        def body(k, carry):
            from_res(source, target, send, recv, k).wait_recv()
            to_res(source, target, send, recv, k).wait_send()
            return carry

        lax.fori_loop(1, res, body, 0)

    moments[r] = moment[...]
    start_res(moment, moments, moment_send, moment_recv)

    middle = tiles // 2
    lax.fori_loop(early, middle, visit_own, 0)

    for copy in halo:
        copy.wait()
    fill_rows(rows, None, moved, atoms, halo_pred, halo_true, halo_kind)
    back[...] = jnp.zeros_like(back)
    for i, j in ((tiles - 2, tiles), (tiles - 1, tiles), (tiles - 1, tiles + 1)):
        for step in spread_steps(split, select, wide, 0, i):
            step()
        near, span = slice(j * TILE, (j + 1) * TILE), slice(i * TILE, (i + 1) * TILE)
        listed = jnp.where(partners[i : i + 1, :] == r * tiles + j, 1.0, 0.0).astype(F32)
        flag = jnp.max(listed, axis=1, keepdims=True)
        sums[5] += masks(rows, near, wide, 0, dist, mask, flag=flag)
        for s in range(copies):
            sums[6 + s] += forces(rows, near, s, wide, 0, dist, mask, force, [])
            back[j - tiles, s] += down(moved, s, span, force)
            acc[i, s] += across(moved, s, near, force)
    returned = pltpu.make_async_remote_copy(
        src_ref=back,
        dst_ref=back_in,
        send_sem=back_send,
        recv_sem=back_recv,
        device_id=(right, v),
        device_id_type=MESH,
    )
    returned.start()
    for step in spread_steps(split, select, wide, middle % 2, middle):
        step()
    lax.fori_loop(middle, tiles, visit_own, 0)
    returned.wait()
    for t in range(BAND):
        acc[t] += back_in[t]

    wait_res(moment, moments, moment_send, moment_recv)
    total = moments[0]
    for k in range(1, res):
        total = total + moments[k]
    turn[0] = total

    def column(a, k):
        picked = turn[0, pl.ds(a, copies, stride=4), :]
        return jnp.broadcast_to(picked[:, k : k + 1], (copies, TILE))

    weight_sum = column(3, 0)
    true_mean = [column(3, 1 + d) / weight_sum for d in range(3)]
    pred_sum = [column(c, 0) for c in range(3)]
    cov = [[column(c, 1 + d) - pred_sum[c] * true_mean[d] for d in range(3)] for c in range(3)]
    square = sum(cov[c][d] * cov[c][d] for c in range(3) for d in range(3))
    frobenius = jnp.sqrt(square)
    polar = tuple(cov[c][d] / frobenius for c in range(3) for d in range(3))

    def sweep(_, flat):
        m = [flat[3 * c : 3 * c + 3] for c in range(3)]
        gram = {}
        for a in range(3):
            for c in range(a, 3):
                gram[a, c] = gram[c, a] = m[a][0] * m[c][0] + m[a][1] * m[c][1] + m[a][2] * m[c][2]
        return tuple(
            1.5 * m[a][d]
            - 0.5 * (gram[a, 0] * m[0][d] + gram[a, 1] * m[1][d] + gram[a, 2] * m[2][d])
            for a in range(3)
            for d in range(3)
        )

    polar = lax.fori_loop(0, 20, sweep, polar)
    for c in range(3):
        for d in range(3):
            turn[1 + d, pl.ds(c, copies, stride=4), :] = polar[3 * c + d]
        turn[4, pl.ds(c, copies, stride=4), :] = pred_sum[c] / weight_sum
        turn[5, pl.ds(c, copies, stride=4), :] = true_mean[c]
    zero = jnp.zeros((1, TILE), F32)
    part[4 + copies :, :] = jnp.zeros((16 - 4 - copies, TILE), F32)
    for s in range(copies):
        spin = [turn[1 + d, 4 * s : 4 * s + 3, :] for d in range(3)]
        mean = [turn[5, 4 * s + d : 4 * s + d + 1, :] for d in range(3)]
        offset = turn[4, 4 * s : 4 * s + 3, :]
        error = jnp.zeros((3, TILE), F32)
        for t in range(tiles):
            span = slice(t * TILE, (t + 1) * TILE)
            target = offset
            for d in range(3):
                target = target + spin[d] * (true[d : d + 1, span] - mean[d])
            away = pred[s, :, span] - target
            scaled = atom_weight(kind[:, span]) * away
            deviation[s, :, span] = scaled
            error = error + scaled * away
        count = 0.5 * sums[0] + sums[5] + inner_sums[0]
        score = 0.5 * count + 0.125 * (0.5 * sums[1 + s] + sums[6 + s] + inner_sums[1 + s])
        part[s : s + 1, :] = jnp.sum(score, axis=0, keepdims=True)
        part[4 + s : 5 + s, :] = jnp.sum(error, axis=0, keepdims=True)
        if s == 0:
            part[8:9, :] = jnp.sum(count, axis=0, keepdims=True)

    parts[r] = part[...]
    start_res(part, parts, part_send, part_recv)
    wait_res(part, parts, part_send, part_recv)
    total = parts[0]
    for k in range(1, res):
        total = total + parts[k]
    total = jnp.broadcast_to(jnp.sum(total, axis=1, keepdims=True), (16, TILE))
    pair_total = total[8:9]
    weight_all = weight_sum[0:1]
    own_loss = zero
    factor = []
    for s in range(copies):
        level = jnp.broadcast_to(noise[0:1, s : s + 1], (1, TILE))
        scale = (level * level + SIGMA * SIGMA) / (level * SIGMA * (level * SIGMA))
        factor.append(scale)
        this = scale * (total[4 + s : 5 + s] / (3.0 * weight_all)) + 1.0 - total[s : s + 1] / pair_total
        copy_loss[s] = this[0, 0]
        own_loss = own_loss + this
    loss[...] = jnp.broadcast_to(own_loss, loss.shape)
    losses[v] = loss[...]

    def to_samp(k):
        return pltpu.make_async_remote_copy(
            src_ref=loss,
            dst_ref=losses.at[v],
            send_sem=loss_send.at[k],
            recv_sem=loss_recv.at[v],
            device_id=(r, lax.rem(v + k, samp)),
            device_id_type=MESH,
        )

    def from_samp(k):
        peer = lax.rem(v + k, samp)
        return pltpu.make_async_remote_copy(
            src_ref=loss,
            dst_ref=losses.at[peer],
            send_sem=loss_send.at[k],
            recv_sem=loss_recv.at[peer],
            device_id=(r, peer),
            device_id_type=MESH,
        )

    def start_samp(k, carry):
        to_samp(k).start()
        return carry

    def wait_samp(k, carry):
        from_samp(k).wait_recv()
        to_samp(k).wait_send()
        return carry

    lax.fori_loop(1, samp, start_samp, 0)

    atom_total = float(atoms * res)
    pull_scale = atom_total / pair_total
    for s in range(copies):
        step_scale = (32.0 * atom_total) * factor[s] / (3.0 * weight_all)
        for t in range(tiles):
            span = slice(t * TILE, (t + 1) * TILE)
            near = acc[t, s]
            pull = (0.5 * pred[s, :, span]) * near[3:4] - near[0:3]
            grad[s, :, span] = step_scale * deviation[s, :, span] + pull_scale * pull

    lax.fori_loop(1, samp, wait_samp, 0)
    whole = losses[0]
    for k in range(1, samp):
        whole = whole + losses[k]
    mean_loss[0] = whole[0, 0] / float(copies * samp)


def shards(res, samp, coords_pred, coords_true, atom_kind, partners, noise_level):
    copies, _, atoms = coords_pred.shape
    tiles = atoms // TILE
    kind = atom_kind.reshape(1, atoms)
    vmem, smem = pl.BlockSpec(memory_space=pltpu.VMEM), pl.BlockSpec(memory_space=pltpu.SMEM)
    spread = [
        pltpu.VMEM((3 * PARTS, PARTS * TILE), BF16),
        pltpu.VMEM((2, TILE, PARTS * TILE), F32),
        pltpu.VMEM((TILE, TILE), F32),
        pltpu.VMEM((TILE, TILE), F32),
        pltpu.VMEM((copies, TILE, 2 * TILE), BF16),
    ]
    inner, inner_sums = pl.pallas_call(
        inner_kernel,
        name="inner_pairs",
        out_shape=(
            jax.ShapeDtypeStruct((tiles, copies, 8, TILE), F32),
            jax.ShapeDtypeStruct((1 + copies, 8, TILE), F32),
        ),
        in_specs=[vmem, vmem, vmem, smem],
        out_specs=(vmem, vmem),
        scratch_shapes=[
            pltpu.VMEM((PARTS, atoms), F32),
            pltpu.VMEM((3 * PARTS, atoms), F32),
            pltpu.VMEM((copies, 32, atoms), BF16),
            *spread,
            pltpu.SMEM((2 * tiles * BAND + 8,), jnp.int32),
        ],
        compiler_params=pltpu.CompilerParams(vmem_limit_bytes=VMEM_BYTES),
    )(coords_pred, coords_true, kind, partners)
    dma = pltpu.SemaphoreType.DMA
    wider = atoms + BAND * TILE
    copy_loss, mean_loss, grad = pl.pallas_call(
        functools.partial(outer_kernel, res, samp),
        name="outer",
        out_shape=(
            jax.ShapeDtypeStruct((copies,), F32),
            jax.ShapeDtypeStruct((1,), F32),
            jax.ShapeDtypeStruct((copies, 3, atoms), F32),
        ),
        in_specs=[vmem] * 7,
        out_specs=(smem, smem, vmem),
        scratch_shapes=[
            pltpu.VMEM((PARTS, wider), F32),
            pltpu.VMEM((copies, 32, wider), BF16),
            pltpu.VMEM((3 * PARTS, atoms), F32),
            *spread,
            pltpu.VMEM((tiles, copies, 8, TILE), F32),
            pltpu.VMEM((2 * (1 + copies), 8, TILE), F32),
            pltpu.VMEM((copies, 3, BAND * TILE), F32),
            pltpu.VMEM((3, BAND * TILE), F32),
            pltpu.VMEM((1, BAND * TILE), jnp.int32),
            pltpu.VMEM((BAND, copies, 8, TILE), F32),
            pltpu.VMEM((BAND, copies, 8, TILE), F32),
            pltpu.VMEM((16, TILE), F32),
            pltpu.VMEM((res, 16, TILE), F32),
            pltpu.VMEM((16, TILE), F32),
            pltpu.VMEM((res, 16, TILE), F32),
            pltpu.VMEM((8, TILE), F32),
            pltpu.VMEM((samp, 8, TILE), F32),
            pltpu.VMEM((6, 16, TILE), F32),
            pltpu.VMEM((copies, 3, atoms), F32),
            dma((3,)),
            dma((3,)),
            dma,
            dma,
            dma((res,)),
            dma((res,)),
            dma((res,)),
            dma((res,)),
            dma((samp,)),
            dma((samp,)),
        ],
        compiler_params=pltpu.CompilerParams(
            collective_id=0, has_side_effects=True, vmem_limit_bytes=VMEM_BYTES
        ),
    )(coords_pred, coords_true, kind, partners, noise_level.reshape(1, copies), inner, inner_sums)
    return (copy_loss, mean_loss.reshape(()), grad)


def solution(mesh):
    in_specs = (P("samp", None, "res"), P(None, "res"), P("res"), P("res", None), P("samp"))
    out_specs = (P("samp"), P(), P("samp", None, "res"))
    body = functools.partial(shards, mesh.shape["res"], mesh.shape["samp"])
    return jax.shard_map(body, mesh=mesh, in_specs=in_specs, out_specs=out_specs, check_vma=False)
```

```python
import functools

import jax
import jax.numpy as jnp
from jax import lax
from jax.experimental import pallas as pl
from jax.experimental.pallas import tpu as pltpu
from jax.sharding import PartitionSpec as P

F32, BF16 = jnp.float32, jnp.bfloat16
MESH = pl.DeviceIdType.MESH
TILE = 128
BAND = 2
CHUNK = 16
COPIES = 4
PARTS = 16
TRUE = 3 * COPIES
LEVELS = (0.25, 0.5, 1.0, 2.0)
UNIT = 2.0**-40
SIGMA = 16.0
VMEM_BYTES = 56 * 1024 * 1024


def lanes(tile, count=1):
    return pl.ds(pl.multiple_of(tile * TILE, TILE), count * TILE)


def row_index(shape):
    return lax.broadcasted_iota(jnp.int32, shape, 0)


def lane_index(shape):
    return lax.broadcasted_iota(jnp.int32, shape, 1)


def atom_weight(kind):
    return jnp.where(kind == 1, 5.0, jnp.where(kind == 2, 10.0, 1.0)).astype(F32)


def pieces(x):
    high = x.astype(BF16).astype(F32)
    mid = (x - high).astype(BF16).astype(F32)
    return high, mid, (x - high) - mid


def fill_rows(rows, moved, at, pred, true, kind):
    width = pred.shape[2]
    span = pl.ds(at, width)
    for t in range(width // TILE):
        block, part = at // TILE + t, slice(t * TILE, (t + 1) * TILE)
        for c in range(3):
            rows[block, COPIES * c : COPIES * (c + 1)] = 0.5 * pred[c, :, part]
        rows[block, TRUE : TRUE + 3] = 0.5 * true[:, part]
        rows[block, TRUE + 3 : TRUE + 4] = jnp.where(kind[:, part] == 1, 15.0, 7.5).astype(F32)
    unit = jnp.where(row_index((5, width)) == 0, 1.0, 0.0).astype(F32)
    for s in range(COPIES):
        half = [0.5 * pred[c, s : s + 1, :] for c in range(3)]
        parts = pieces(jnp.concatenate([*half, unit], axis=0))
        stack = jnp.concatenate([*parts, jnp.zeros((8, width), F32)], axis=0)
        moved[s, :, span] = stack.astype(BF16)


def fill_turned(turned, rows, tiles):
    def one(t, carry):
        turned[t] = jnp.transpose(jnp.concatenate(pieces(rows[t]), axis=0)).astype(BF16)
        return carry

    lax.fori_loop(0, tiles, one, 0, unroll=4)


def fill_select(select):
    row, column = row_index(select.shape) % PARTS, lane_index(select.shape) // TILE
    select[...] = jnp.where(row == column, 1.0, 0.0).astype(BF16)


def spread_values(turned, select, tile, quarter):
    return jnp.dot(turned[tile], select[:, wide_block(quarter)], preferred_element_type=F32)


def mask_rows(rows, near, wide, dist, mask, less, band, own, flag):
    cut = rows[near, TRUE + 3 : TRUE + 4]

    def wide_row(r):
        return wide[band, r * TILE : (r + 1) * TILE]

    gap = [wide_row(TRUE + c) - rows[near, TRUE + c : TRUE + c + 1] for c in range(3)]
    square = gap[0] * gap[0] + gap[1] * gap[1] + (gap[2] * gap[2] + 2.5e-7)
    length = square * lax.rsqrt(square)
    both = jnp.where(length < cut, UNIT, 0.0) + jnp.where(length < wide_row(TRUE + 3), UNIT, 0.0)
    if own is not None:
        shape = (band.stop - band.start, TILE)
        same = (row_index(shape) + band.start) - lane_index(shape) == own
        both = jnp.where(same, 0.0, both * flag)
    dist[band] = length
    mask[band] = both
    less[band] = -both
    return sum(both[v : v + 8] for v in range(0, band.stop - band.start, 8))


def forces(rows, near, s, wide, dist, mask, less, high, low):
    mate = [rows[near, COPIES * c + s : COPIES * c + s + 1] for c in range(3)]
    total = jnp.zeros((8, TILE), F32)
    for start in range(0, TILE, CHUNK):
        band = slice(start, start + CHUNK)
        gap = [wide[band, (COPIES * c + s) * TILE : (COPIES * c + s + 1) * TILE] - mate[c] for c in range(3)]
        square = gap[0] * gap[0] + gap[1] * gap[1] + (gap[2] * gap[2] + 2.5e-7)
        inverse = lax.rsqrt(square)
        excess = square * inverse - dist[band]
        spread = jnp.abs(excess)
        th = [jnp.tanh(level - spread) for level in LEVELS]
        both = mask[band]
        score = both * ((th[0] + th[1]) + (th[2] + th[3]))
        for v in range(0, CHUNK, 8):
            total += score[v : v + 8]
        slope = 4.0 - ((th[0] * th[0] + th[1] * th[1]) + (th[2] * th[2] + th[3] * th[3]))
        signed = jnp.minimum(jnp.maximum(excess, less[band]), both)
        pull = (signed * inverse) * slope
        top = pull.astype(BF16)
        high[s, band] = top
        low[s, band] = (pull - top.astype(F32)).astype(BF16)
    return total


def fold(x):
    return (x[0:8] + x[8:16]) + x[16:24]


def gather_pulls(acc, moved, high, low, g, q, s):
    at = slice(8 * s, 8 * (s + 1))
    here, near = moved[s, :, lanes(g)], moved[s, :, lanes(q)]
    both = jnp.concatenate([high[s], low[s]], axis=1)
    out = jnp.dot(here, both, preferred_element_type=F32)
    across = (((1,), (1,)), ((), ()))
    back = lax.dot_general(near, high[s], across, preferred_element_type=F32)
    back = back + lax.dot_general(near, low[s], across, preferred_element_type=F32)
    acc[q, at] += fold(out[:, 0:TILE] + out[:, TILE : 2 * TILE])
    acc[g, at] += fold(back)


def pair_loop(count, exact, item, weigh, hook, rows, moved, turned, select, wide, dist, mask, less, high, low, acc, sums):
    quarter_rows = TILE // COPIES

    def masked(tile, weight, k, quarter):
        own, flag, live = weight
        band = slice(quarter * quarter_rows, (quarter + 1) * quarter_rows)
        part = mask_rows(rows, tile, wide[k], dist[k], mask[k], less[k], band, own, flag)
        sums[0] += part if live is None else live * part

    for ref in (high[2], low[2]):
        ref[...] = jnp.zeros_like(ref)
    for p in range(2):
        for quarter in range(COPIES):
            wide[p][:, wide_block(quarter)] = spread_values(turned, select, item(p)[0], quarter)
    for quarter in range(COPIES):
        masked(item(0)[1], weigh(0), 0, quarter)

    def visit(p, k, g_before, q_before):
        g, q = item(p)
        q_next, g_later = item(p + 1)[1], item(p + 2)[0]
        weight_next = weigh(p + 1)
        following, ahead = (k + 1) % 3, (k + 2) % 3
        for s in range(COPIES):
            gather_pulls(acc, moved, high[ahead], low[ahead], g_before, q_before, s)
            wide[ahead][:, wide_block(s)] = spread_values(turned, select, g_later, s)
            sums[1 + s] += forces(
                rows, q, s, wide[k], dist[k], mask[k], less[k], high[k], low[k]
            )
            masked(q_next, weight_next, following, s)

    def three(turn, before):
        for k in range(3):
            p = 3 * turn + k
            hook(p)
            if exact:
                visit(p, k, *before)
            else:
                pl.when(p < count)(functools.partial(visit, p, k, *before))
            before = item(p)
        return before

    first = tuple(jnp.asarray(t, jnp.int32) for t in item(0))
    lax.fori_loop(0, (count + 2) // 3, three, first)
    g, q = item(lax.max(count - 1, 0))

    def finish(k):
        for s in range(COPIES):
            gather_pulls(acc, moved, high[k], low[k], g, q, s)

    if exact:
        finish(2)
    else:
        for k in range(3):
            pl.when(lax.rem(count + 2, 3) == k)(functools.partial(finish, k))


def wide_block(quarter):
    return slice(quarter * 4 * TILE, (quarter + 1) * 4 * TILE)


def inner_kernel(pred, true, kind, partners, acc, sums, rows, moved, turned, select, wide, dist, mask, less, high, low, pairs):
    tiles = pred.shape[2] // TILE
    first = lax.axis_index("res") * tiles

    def look(g, n):
        for k in range(1, partners.shape[0]):
            q = partners[k, g] - first
            pairs[n] = g
            pairs[n + 1] = q
            n = n + jnp.where((q > g) & (q < tiles), 2, 0)
        return n

    end = lax.fori_loop(0, tiles, look, 0)
    for k in range(10):
        pairs[end + k] = 0
    count = end // 2
    fill_rows(rows, moved, 0, pred, true, kind)
    fill_turned(turned, rows, tiles)
    fill_select(select)
    acc[...] = jnp.zeros_like(acc)
    sums[...] = jnp.zeros_like(sums)

    def item(p):
        return pairs[2 * p], pairs[2 * p + 1]

    def weigh(p):
        return None, None, jnp.where(p < count, 1.0, 0.0).astype(F32)

    pair_loop(
        count, False, item, weigh, lambda p: None, rows, moved, turned, select, wide, dist, mask, less, high, low, acc, sums
    )


def outer_kernel(
    res,
    samp,
    pred,
    true,
    kind,
    partners,
    noise,
    inner,
    inner_sums,
    copy_loss,
    mean_loss,
    grad,
    rows,
    moved,
    turned,
    select,
    wide,
    dist,
    mask,
    less,
    high,
    low,
    acc,
    sums,
    halo_pred,
    halo_true,
    halo_kind,
    back_in,
    moment,
    moments,
    part,
    parts,
    loss,
    losses,
    deviation,
    halo_send,
    halo_recv,
    back_send,
    back_recv,
    moment_send,
    moment_recv,
    part_send,
    part_recv,
    loss_send,
    loss_recv,
):
    atoms = pred.shape[2]
    tiles = atoms // TILE
    r, v = lax.axis_index("res"), lax.axis_index("samp")
    left, right = lax.rem(r + res - 1, res), lax.rem(r + 1, res)
    barrier = pltpu.get_barrier_semaphore()

    def along_res(k):
        return (lax.rem(r + k, res), v)

    def along_samp(k):
        return (r, lax.rem(v + k, samp))

    def each(count, do):
        def body(k, carry):
            do(k)
            return carry

        lax.fori_loop(1, count, body, 0)

    def greet(where):
        return lambda k: pl.semaphore_signal(
            barrier, inc=1, device_id=where(k), device_id_type=MESH
        )

    each(res, greet(along_res))
    each(samp, greet(along_samp))

    def shared(source, target, send, recv, where, axis, count, me):
        def copy(k, slot):
            return pltpu.make_async_remote_copy(
                src_ref=source,
                dst_ref=target.at[slot],
                send_sem=send.at[k],
                recv_sem=recv.at[slot],
                device_id=where(k),
                device_id_type=MESH,
            )

        def start():
            each(count, lambda k: copy(k, me).start())

        def wait():
            def one(k):
                copy(k, where(k)[axis]).wait_recv()
                copy(k, me).wait_send()

            each(count, one)

        return start, wait

    start_moment, wait_moment = shared(
        moment, moments, moment_send, moment_recv, along_res, 0, res, r
    )
    start_part, wait_part = shared(part, parts, part_send, part_recv, along_res, 0, res, r)
    start_loss, wait_loss = shared(loss, losses, loss_send, loss_recv, along_samp, 1, samp, v)

    edge = pl.ds(0, BAND * TILE)
    halo = [
        pltpu.make_async_remote_copy(
            src_ref=source,
            dst_ref=target,
            send_sem=halo_send.at[k],
            recv_sem=halo_recv.at[k],
            device_id=(left, v),
            device_id_type=MESH,
        )
        for k, (source, target) in enumerate(
            [
                (pred.at[:, :, edge], halo_pred),
                (true.at[:, edge], halo_true),
                (kind.at[:, edge], halo_kind),
            ]
        )
    ]
    returned = pltpu.make_async_remote_copy(
        src_ref=acc.at[pl.ds(tiles, BAND)],
        dst_ref=back_in,
        send_sem=back_send,
        recv_sem=back_recv,
        device_id=(right, v),
        device_id_type=MESH,
    )

    fill_rows(rows, moved, 0, pred, true, kind)
    fill_turned(turned, rows, tiles)
    turned[tiles : tiles + BAND] = jnp.zeros((BAND, TILE, 3 * PARTS), BF16)
    fill_select(select)
    weight = atom_weight(kind[...])
    last = row_index((PARTS, TILE)) == PARTS - 1
    columns = [jnp.zeros((PARTS, TILE), F32) for k in range(4)]
    for t in range(tiles):
        span = slice(t * TILE, (t + 1) * TILE)
        block = jnp.where(last, 0.5, rows[t])
        for k in range(4):
            by = weight[:, span] if k == 0 else weight[:, span] * true[k - 1 : k, span]
            columns[k] = columns[k] + block * by
    packed = jnp.zeros((PARTS, TILE), F32)
    for k in range(4):
        column = 2.0 * jnp.sum(columns[k], axis=1, keepdims=True)
        packed = jnp.where(lane_index((PARTS, TILE)) == k, column, packed)
    moment[...] = packed
    moments[r] = packed
    acc[0:tiles] = inner[...]
    acc[tiles : tiles + BAND] = jnp.zeros((BAND, 8 * COPIES, TILE), F32)
    sums[...] = inner_sums[...]

    def item(p):
        far = p // tiles
        k = p - tiles
        return (
            (1 - far) * p + far * (tiles - 2 + (k + 1) // 2),
            (1 - far) * p + far * (tiles + k // 2),
        )

    listed = []
    for i, j in ((tiles - 2, tiles), (tiles - 1, tiles), (tiles - 1, tiles + 1)):
        found = jnp.where(partners[:, i : i + 1] == r * tiles + j, 1.0, 0.0).astype(F32)
        listed.append(jnp.broadcast_to(jnp.max(found, axis=0, keepdims=True), (1, TILE)))

    def weigh(p):
        far = p // tiles
        own = far * (4 * TILE)
        flag = jnp.where(p < tiles, 0.5, 0.0).astype(F32)
        for k in range(3):
            flag = jnp.where(p == tiles + k, listed[k], flag)
        return own, flag, None

    opened, entered = tiles // 4, tiles // 2

    def hook(p):
        @pl.when(p == opened)
        def _():
            pl.semaphore_wait(barrier, res - 1 + samp - 1)
            for copy in halo:
                copy.start()
            start_moment()

        @pl.when(p == entered)
        def _():
            for copy in halo:
                copy.wait()
            fill_rows(rows, moved, atoms, halo_pred, halo_true, halo_kind)

    pair_loop(
        tiles + 3, (tiles + 3) % 3 == 0, item, weigh, hook, rows, moved, turned, select, wide, dist, mask, less, high, low, acc, sums
    )
    returned.start()

    wait_moment()
    total = moments[0]
    for k in range(1, res):
        total = total + moments[k]

    def column(c, k):
        rows_of = slice(COPIES * c, COPIES * (c + 1))
        return jnp.broadcast_to(total[rows_of, k : k + 1], (COPIES, TILE))

    def alone(row):
        return jnp.broadcast_to(total[row : row + 1, 0:1], (COPIES, TILE))

    weight_sum = alone(PARTS - 1)
    true_mean = [alone(TRUE + d) / weight_sum for d in range(3)]
    pred_sum = [column(c, 0) for c in range(3)]
    pred_mean = [pred_sum[c] / weight_sum for c in range(3)]
    cov = [[column(c, 1 + d) - pred_sum[c] * true_mean[d] for d in range(3)] for c in range(3)]
    square = sum(cov[c][d] * cov[c][d] for c in range(3) for d in range(3))
    frobenius = jnp.sqrt(square)
    polar = tuple(cov[c][d] / frobenius for c in range(3) for d in range(3))

    def sweep(_, flat):
        m = [flat[3 * c : 3 * c + 3] for c in range(3)]
        gram = {}
        for a in range(3):
            for c in range(a, 3):
                gram[a, c] = gram[c, a] = m[a][0] * m[c][0] + m[a][1] * m[c][1] + m[a][2] * m[c][2]
        return tuple(
            1.5 * m[a][d]
            - 0.5 * (gram[a, 0] * m[0][d] + gram[a, 1] * m[1][d] + gram[a, 2] * m[2][d])
            for a in range(3)
            for d in range(3)
        )

    polar = lax.fori_loop(0, 20, sweep, polar)
    error = jnp.zeros((COPIES, TILE), F32)
    for t in range(tiles):
        span = slice(t * TILE, (t + 1) * TILE)
        heavy = atom_weight(kind[:, span])
        centred = [true[d : d + 1, span] - true_mean[d] for d in range(3)]
        for c in range(3):
            turned_row = polar[3 * c : 3 * c + 3]
            target = (
                turned_row[0] * centred[0] + turned_row[1] * centred[1] + turned_row[2] * centred[2]
            ) + pred_mean[c]
            away = pred[c, :, span] - target
            scaled = heavy * away
            deviation[c, :, span] = scaled
            error = error + scaled * away
    count = sums[0] / UNIT
    scores = [
        jnp.sum(0.5 * count + (0.125 / UNIT) * sums[1 + s], axis=0, keepdims=True) for s in range(COPIES)
    ]
    counted = jnp.broadcast_to(jnp.sum(count, axis=0, keepdims=True), (PARTS - 2 * COPIES, TILE))
    summed = jnp.concatenate([*scores, error, counted], axis=0)
    part[...] = summed
    parts[r] = summed
    start_part()
    returned.wait()
    for t in range(BAND):
        acc[t] += back_in[t]
    wait_part()
    total = parts[0]
    for k in range(1, res):
        total = total + parts[k]
    total = jnp.sum(total, axis=1, keepdims=True)
    pair_total = jnp.broadcast_to(total[2 * COPIES : 2 * COPIES + 1], (COPIES, TILE))
    score_total = jnp.broadcast_to(total[0:COPIES], (COPIES, TILE))
    square_err = jnp.broadcast_to(total[COPIES : 2 * COPIES], (COPIES, TILE))
    square_shape = (COPIES, COPIES)
    level = jnp.sum(
        jnp.where(
            row_index(square_shape) == lane_index(square_shape),
            jnp.broadcast_to(noise[...], square_shape),
            0.0,
        ),
        axis=1,
        keepdims=True,
    )
    level = jnp.broadcast_to(level, (COPIES, TILE))
    factor = (level * level + SIGMA * SIGMA) / (level * SIGMA * (level * SIGMA))
    lost = factor * (square_err / (3.0 * weight_sum)) + 1.0 - score_total / pair_total
    sent = jnp.broadcast_to(jnp.sum(lost, axis=0, keepdims=True), loss.shape)
    loss[...] = sent
    losses[v] = sent
    start_loss()
    for s in range(COPIES):
        copy_loss[s] = lost[s, 0]

    atom_total = float(atoms * res)
    pull_scale = (atom_total / UNIT) / pair_total
    step_scale = (32.0 * atom_total) * factor / (3.0 * weight_sum)
    for t in range(tiles):
        span = slice(t * TILE, (t + 1) * TILE)
        sum_of = [acc[t, pl.ds(c, COPIES, stride=8), :] for c in range(4)]
        for c in range(3):
            pull = (0.5 * pred[c, :, span]) * sum_of[3] - sum_of[c]
            grad[c, :, span] = step_scale * deviation[c, :, span] + pull_scale * pull

    wait_loss()
    whole = losses[0]
    for k in range(1, samp):
        whole = whole + losses[k]
    mean_loss[0] = whole[0, 0] / float(COPIES * samp)


def shards(res, samp, coords_pred, coords_true, atom_kind, partners, noise_level):
    copies, _, atoms = coords_pred.shape
    assert copies == COPIES
    tiles = atoms // TILE
    pred = jnp.transpose(coords_pred, (1, 0, 2))
    kind = atom_kind.reshape(1, atoms)
    listed = jnp.transpose(partners)
    vmem, smem = pl.BlockSpec(memory_space=pltpu.VMEM), pl.BlockSpec(memory_space=pltpu.SMEM)
    wider = atoms + BAND * TILE

    def work(width):
        return [
            pltpu.VMEM((width // TILE, PARTS, TILE), F32),
            pltpu.VMEM((COPIES, 32, width), BF16),
            pltpu.VMEM((tiles + BAND, TILE, 3 * PARTS), BF16),
            pltpu.VMEM((3 * PARTS, PARTS * TILE), BF16),
            tuple(pltpu.VMEM((TILE, PARTS * TILE), F32) for _ in range(3)),
            *(tuple(pltpu.VMEM((TILE, TILE), F32) for _ in range(3)) for _ in range(3)),
            *(tuple(pltpu.VMEM((COPIES, TILE, TILE), BF16) for _ in range(3)) for _ in range(2)),
        ]

    inner, inner_sums = pl.pallas_call(
        inner_kernel,
        name="inner_pairs",
        out_shape=(
            jax.ShapeDtypeStruct((tiles, 8 * COPIES, TILE), F32),
            jax.ShapeDtypeStruct((1 + COPIES, 8, TILE), F32),
        ),
        in_specs=[vmem, vmem, vmem, smem],
        out_specs=(vmem, vmem),
        scratch_shapes=[*work(atoms), pltpu.SMEM((2 * tiles * BAND + 16,), jnp.int32)],
        compiler_params=pltpu.CompilerParams(vmem_limit_bytes=VMEM_BYTES),
    )(pred, coords_true, kind, listed)
    dma = pltpu.SemaphoreType.DMA
    copy_loss, mean_loss, grad = pl.pallas_call(
        functools.partial(outer_kernel, res, samp),
        name="outer",
        out_shape=(
            jax.ShapeDtypeStruct((COPIES,), F32),
            jax.ShapeDtypeStruct((1,), F32),
            jax.ShapeDtypeStruct((3, COPIES, atoms), F32),
        ),
        in_specs=[vmem] * 7,
        out_specs=(smem, smem, vmem),
        scratch_shapes=[
            *work(wider),
            pltpu.VMEM((tiles + BAND, 8 * COPIES, TILE), F32),
            pltpu.VMEM((1 + COPIES, 8, TILE), F32),
            pltpu.VMEM((3, COPIES, BAND * TILE), F32),
            pltpu.VMEM((3, BAND * TILE), F32),
            pltpu.VMEM((1, BAND * TILE), jnp.int32),
            pltpu.VMEM((BAND, 8 * COPIES, TILE), F32),
            pltpu.VMEM((PARTS, TILE), F32),
            pltpu.VMEM((res, PARTS, TILE), F32),
            pltpu.VMEM((PARTS, TILE), F32),
            pltpu.VMEM((res, PARTS, TILE), F32),
            pltpu.VMEM((8, TILE), F32),
            pltpu.VMEM((samp, 8, TILE), F32),
            pltpu.VMEM((3, COPIES, atoms), F32),
            dma((3,)),
            dma((3,)),
            dma,
            dma,
            dma((res,)),
            dma((res,)),
            dma((res,)),
            dma((res,)),
            dma((samp,)),
            dma((samp,)),
        ],
        compiler_params=pltpu.CompilerParams(
            collective_id=0, has_side_effects=True, vmem_limit_bytes=VMEM_BYTES
        ),
    )(pred, coords_true, kind, listed, noise_level.reshape(1, COPIES), inner, inner_sums)
    return (copy_loss, mean_loss.reshape(()), jnp.transpose(grad, (1, 0, 2)))


def solution(mesh):
    in_specs = (P("samp", None, "res"), P(None, "res"), P("res"), P("res", None), P("samp"))
    out_specs = (P("samp"), P(), P("samp", None, "res"))
    body = functools.partial(shards, mesh.shape["res"], mesh.shape["samp"])
    return jax.shard_map(body, mesh=mesh, in_specs=in_specs, out_specs=out_specs, check_vma=False)
```
